512 devices in a mesh: gx: 16 (over z, core), gy: 32 (over x, y).
Axes of the slice: x: 4, y: 8, z: 8, core: 2. Of those that a mesh axis runs over, the one named last changes fastest.
Arguments:
- control: float32 [16, 4096, 2048], P(None, 'gy', 'gx'), may hold values from -6 to 6
- scale_x: float32 [16, 2048], replicated, may hold values from 2 to 384
- scale_y: float32 [16, 4096], P(None, 'gy'), may hold values from 2 to 384
- vertical_taps: float32 [5, 16], replicated, may hold values from 0.1 to 0.5
Outputs:
- increment: float32 [16, 4096, 2048], P(None, 'gy', 'gx')
The draws below stay inside these ranges and needn't reach their ends.
All inputs are finite; a program needn't handle non-finite values.
Results may differ from the reference program's by a relative error of at most 0.00016.
Values sent between devices are 32-bit elements; how exact they have to be, the bound alone decides.
No kernel may reach another device: no remote copies, remote signals or barrier semaphores. Data moves between devices by JAX's collectives and lax.ppermute only.
A program may use at most 64 MiB of HBM per device.

```python
import math
import jax
import jax.numpy as jnp
from jax import lax

L = 16
CX = 128
CY = 128
NX = 2048
NY = 4096


def level_base(key, count, upper):
    order = jax.random.permutation(jax.random.fold_in(key, 11), count)
    rank = order.astype(jnp.float32) / float(max(count - 1, 1))
    return 3.5 * jnp.power(jnp.float32(upper / 3.5), rank)


def spread_factor(key, count, length):
    return jnp.exp(jax.random.uniform(jax.random.fold_in(key, 23), (count, length), jnp.float32, math.log(0.7), math.log(1.4)))


def draw_scale_x(key, part):
    own_key = jax.random.fold_in(key, 101)
    base = level_base(own_key, L, 2.0 * CX)
    factor = spread_factor(own_key, L, NX)
    return (base[:, None] * factor).astype(jnp.float32)


def draw_scale_y(key, part):
    own_key = jax.random.fold_in(key, 202)
    base = level_base(own_key, L, 2.0 * CY)
    factor = spread_factor(own_key, L, NY)
    return (base[:, None] * factor).astype(jnp.float32)


def level_of(key, dims, shards, low, high):
    level, own = 1.0, jax.random.fold_in(key, 6)
    for dim, parts in shards:
        heights = jnp.exp(jax.random.uniform(jax.random.fold_in(own, dim), (parts,), jnp.float32, low / len(shards), high / len(shards)))
        level = level * jnp.repeat(heights, dims[dim] // parts).reshape([-1 if axis == dim else 1 for axis in range(len(dims))])
    return level


def noise(stream_key, dims, scale, most, split=(), held_as=jnp.bfloat16):
    values = scale * jax.random.normal(stream_key, dims, jnp.float32)
    if split:
        values = values * level_of(stream_key, dims, split, -0.22, 0.18)
    return jnp.clip(values, -most, most).astype(held_as)


def setup_inputs(seed: int = 0) -> dict:
    splits = jax.random.split(jax.random.key(seed), 5)
    control = noise(splits[0], (L, NY, NX), 1.0, 6.0, ((1, 32), (2, 16)), jnp.float32)
    scale_x = draw_scale_x(jax.random.fold_in(splits[4], 71), 0)
    scale_y = draw_scale_y(jax.random.fold_in(splits[4], 71), 0)
    vertical_taps = jnp.clip(jax.random.uniform(splits[3], (5, L), jnp.float32, 0.1, 0.5), 0.1, 0.5)
    return {"control": control, "scale_x": scale_x, "scale_y": scale_y, "vertical_taps": vertical_taps}


def sweep_last(values, damping):
    moved = jnp.moveaxis(values, 2, 0)
    poles_first = jnp.moveaxis(damping, 1, 0)

    def advance(states, item):
        inflow, factor = item
        factor = factor[:, None]
        first = factor * states[0] + (1.0 - factor) * inflow
        second = factor * states[1] + (1.0 - factor) * first
        third = factor * states[2] + (1.0 - factor) * second
        fourth = factor * states[3] + (1.0 - factor) * third
        return ((first, second, third, fourth), fourth)
    blanks = jnp.zeros(moved.shape[1:], jnp.float32)
    _, result = lax.scan(advance, (blanks, blanks, blanks, blanks), (moved, poles_first))
    return jnp.moveaxis(result, 0, 2)

def both_ways(values, damping):
    forward = sweep_last(values, damping)
    return jnp.flip(sweep_last(jnp.flip(forward, 2), jnp.flip(damping, 1)), 2)

def reference(control, scale_x, scale_y, vertical_taps):
    pole_x = jnp.exp(-1.0 / scale_x)
    pole_y = jnp.exp(-1.0 / scale_y)
    values = control * jnp.sqrt(8.0 * scale_x)[:, None, :]
    values = both_ways(values, pole_x)
    values = values * jnp.sqrt(8.0 * scale_y)[:, :, None]
    turned = jnp.swapaxes(values, 1, 2)
    turned = both_ways(turned, pole_y)
    values = jnp.swapaxes(turned, 1, 2)
    levels = values.shape[0]
    padded = jnp.pad(values, ((2, 2), (0, 0), (0, 0)))
    increment = jnp.zeros_like(values)
    for offset in range(5):
        increment = increment + vertical_taps[offset][:, None, None] * padded[offset:offset + levels]
    return increment
```

```python
import functools
import jax
import jax.numpy as jnp
from jax import lax
from jax.experimental import pallas as pl
from jax.experimental.pallas import tpu as pltpu
from jax.sharding import PartitionSpec as P


F32 = jnp.float32
BF16 = jnp.bfloat16
N = 128
HALF = 64
GRANT = 16 << 20


def split(a):
    high = a.astype(BF16)
    return high, (a - high.astype(F32)).astype(BF16)


def dot3(a, b, dims):
    ah, al = a if isinstance(a, tuple) else split(a)
    bh, bl = b if isinstance(b, tuple) else split(b)

    def one(u, v):
        return lax.dot_general(u, v, (dims, ((), ())), preferred_element_type=F32)

    return one(ah, bh) + (one(ah, bl) + one(al, bh))


NN = ((1,), (0,))
NT = ((1,), (1,))
TN = ((0,), (0,))


def poly(a, b):
    out = []
    for k in range(4):
        total = a[0] * b[k]
        for m in range(1, k + 1):
            total = total + a[m] * b[k - m]
        out.append(total)
    return out


def geometric(lead, q):
    out = [lead]
    for _ in range(3):
        out.append(out[-1] * q)
    return out


def sym(table, a, b):
    return table[(max(a, b), min(a, b))]


def congruence(t, r):
    x = {}
    for c in range(4):
        for a in range(4):
            total = t[0] * sym(r, a, c)
            for m in range(1, a + 1):
                total = total + t[m] * sym(r, a - m, c)
            x[(a, c)] = total
    out = {}
    for a in range(4):
        for b in range(a + 1):
            total = t[0] * x[(a, b)]
            for m in range(1, b + 1):
                total = total + t[m] * x[(a, b - m)]
            out[(a, b)] = total
    return out


def lanes(shape):
    return lax.broadcasted_iota(jnp.int32, shape, len(shape) - 1)


def later(x, d, fill):
    moved = pltpu.roll(x, N - d, 1)
    return jnp.where(lanes(x.shape) < N - d, moved, fill)


def earlier(x, d, fill):
    moved = pltpu.roll(x, d, 1)
    return jnp.where(lanes(x.shape) >= d, moved, fill)


def ones_first(k):
    return 1.0 if k == 0 else 0.0


def poles(scale):
    p = jnp.exp(-1.0 / scale)
    return p, 1.0 - p


def suffix_scan(p, q):
    t = geometric(p, q)
    g = [p * q]
    for _ in range(6):
        g.append(g[-1] * q)
    r = {(a, b): g[a + b] for a in range(4) for b in range(a + 1)}
    d = 1
    while d < N:
        t2 = [later(t[k], d, ones_first(k)) for k in range(4)]
        r2 = {key: later(value, d, 0.0) for key, value in r.items()}
        grown = congruence(t, r2)
        r = {key: r[key] + grown[key] for key in r}
        t = poly(t, t2)
        d *= 2
    return t, r


def prefix_scan(p, q):
    t = geometric(p, q)
    d = 1
    while d < N:
        t = poly(t, [earlier(t[k], d, ones_first(k)) for k in range(4)])
        d *= 2
    return t


def return_map(r, s):
    out = []
    for a in range(4):
        total = sym(r, a, 3) * s[0]
        for b in range(1, 4):
            total = total + sym(r, a, 3 - b) * s[b]
        out.append(total)
    return out


def extraction(p, q, t, r, before):
    inject = geometric(q, q)
    t_next = [later(t[k], 1, ones_first(k)) for k in range(4)]
    r_next = {key: later(value, 1, 0.0) for key, value in r.items()}
    f = poly(t_next, inject)
    back = poly(geometric(p, q), return_map(r_next, inject))
    back = [back[k] + inject[k] * inject[3] for k in range(4)]
    px = [earlier(before[k], 1, ones_first(k)) for k in range(4)]
    return f, poly(px, back)


def response(t, r, before):
    px = [earlier(before[k], 1, ones_first(k)) for k in range(4)]
    out = []
    for k in range(4):
        total = sym(r, 3, 3 - k) * px[0]
        for b in range(k + 1, 4):
            total = total + sym(r, 3, 3 - b) * px[b - k]
        out.append(total)
    return out + [t[3 - k] for k in range(4)]


COEFS = [(a, b) for a in range(4) for b in range(a + 1)]


def own_scale(axis, scale_ref):
    if axis is None:
        return scale_ref[...]
    me = lax.axis_index(axis)
    return scale_ref[:, pl.ds(pl.multiple_of(me * N, N), N)]


def states_x_kernel(scale_ref, control_ref, out_ref, weights):
    scale = own_scale("gx", scale_ref)
    p, q = poles(scale)
    t, r = suffix_scan(p, q)
    before = prefix_scan(p, q)
    f, b = extraction(p, q, t, r, before)
    amplitude = jnp.sqrt(8.0 * scale)
    for k in range(4):
        weights[:, k, :] = f[k] * amplitude
        weights[:, 4 + k, :] = b[k] * amplitude
    for level in range(out_ref.shape[0]):
        out_ref[level] = dot3(weights[level], control_ref[level], NT)


def link_x_kernel(scale_ref, out_ref, gathered, spread):
    blocks = out_ref.shape[0] // 8
    me = lax.axis_index("gx")
    level = lax.broadcasted_iota(jnp.int32, (scale_ref.shape[0], N), 0)
    for j in range(blocks):
        block = jnp.where(level == me, scale_ref[:, j * N:(j + 1) * N], 0.0)
        gathered[j:j + 1, :] = jnp.sum(block, axis=0, keepdims=True)
    p, q = poles(gathered[...])
    t, r = suffix_scan(p, q)
    for k in range(4):
        spread[k] = jnp.broadcast_to(t[k][:, 0:1], (blocks, N))
    for m, key in enumerate(COEFS):
        spread[4 + m] = jnp.broadcast_to(r[key][:, 0:1], (blocks, N))
    lane = lanes((1, N))
    run_links(
        blocks,
        lambda j, k: (lane == 8 * j + k).astype(F32),
        spread,
        lambda j, k, value: out_ref.__setitem__((pl.ds(8 * j + k, 1), slice(None)), value),
    )


def run_links(blocks, source, spread, store):
    zero = jnp.zeros((1, N), F32)
    s = [zero] * 4
    returns = []
    for j in range(blocks):
        t = [spread[k, j:j + 1, :] for k in range(4)]
        r = {key: spread[4 + m, j:j + 1, :] for m, key in enumerate(COEFS)}
        for k in range(4):
            store(j, k, s[k])
        back = return_map(r, s)
        returns.append([back[k] + source(j, 4 + k) for k in range(4)])
        moved = poly(t, s)
        s = [moved[k] + source(j, k) for k in range(4)]
    e = [zero] * 4
    for j in reversed(range(blocks)):
        t = [spread[k, j:j + 1, :] for k in range(4)]
        for k in range(4):
            store(j, 4 + k, e[k])
        moved = poly(t, e)
        e = [moved[k] + returns[j][k] for k in range(4)]


def apply_x_kernel(link_ref, states_ref, out_ref):
    blocks = out_ref.shape[0]
    flat = states_ref[...].reshape(blocks * 8, N)
    out_ref[...] = dot3(link_ref[...], flat, NN).reshape(blocks, 8, N)


def filter_kernel(axis, scale_ref, local_ref, spread, middle):
    scale = own_scale(axis, scale_ref)
    levels = scale.shape[0]
    p, q = poles(scale)
    for i in range(N):
        spread[i] = jnp.broadcast_to(p[:, i:i + 1], (levels, N))
    shape = (levels, N)
    lane = lanes(shape)
    zero = jnp.zeros(shape, F32)
    column = jnp.sqrt(8.0 * scale) if axis is None else p / q

    def advance(factor, state, inflow):
        rest = 1.0 - factor
        out = []
        for k in range(4):
            inflow = factor * state[k] + rest * inflow
            out.append(inflow)
        return out

    def forward(i, state):
        state = advance(spread[i], state, (lane == i).astype(F32))
        middle[i] = state[3]
        return tuple(state)

    lax.fori_loop(0, N, forward, (zero,) * 4, unroll=8)

    def backward(k, state):
        i = N - 1 - k
        state = advance(spread[i], state, middle[i])
        local_ref[:, pl.ds(i, 1), :] = (state[3] * column).reshape(levels, 1, N)
        return tuple(state)

    lax.fori_loop(0, N, backward, (zero,) * 4, unroll=8)


def tables_kernel(scale_x_ref, scale_y_ref, entry_x_ref, gain_x_ref, extract_ref, entry_y_ref, coef_ref):
    levels = scale_y_ref.shape[0]
    scale = jnp.concatenate([own_scale("gx", scale_x_ref), scale_y_ref[...]], 0)
    p, q = poles(scale)
    t, r = suffix_scan(p, q)
    before = prefix_scan(p, q)
    amplitude = jnp.sqrt(8.0 * scale)
    gain_x_ref[...] = (amplitude * q / p)[:levels]
    for k, row in enumerate(response(t, r, before)):
        entry_x_ref[:, k, :] = row[:levels]
        entry_y_ref[:, k, :] = row[levels:]
    p, q, amplitude = p[levels:], q[levels:], amplitude[levels:]
    t = [value[levels:] for value in t]
    r = {key: value[levels:] for key, value in r.items()}
    f, b = extraction(p, q, t, r, [value[levels:] for value in before])
    for k in range(4):
        extract_ref[:, k, :] = f[k] * amplitude
        extract_ref[:, 4 + k, :] = b[k] * amplitude
    shape = p.shape
    lane = lanes(shape)
    coefs = jnp.zeros(shape, F32)
    for m, value in enumerate(t + [r[key] for key in COEFS]):
        coefs = jnp.where(lane == HALF + m, jnp.broadcast_to(value[:, 0:1], shape), coefs)
    coef_ref[...] = coefs


def local_x_kernel(control_ref, gain_ref, filter_ref, extract_ref, out_ref, base_ref):
    for level in range(out_ref.shape[0]):
        g = dot3(control_ref[level] * gain_ref[level:level + 1, :], filter_ref[level], NN)
        out_ref[level] = g
        base_ref[level] = dot3(extract_ref[level], g, NN)


def states_y_kernel(enter_ref, entry_ref, extract_ref, base_ref, coef_ref, out_ref):
    left = lanes((8, N)) < HALF
    for level in range(base_ref.shape[0]):
        corner = dot3(extract_ref[level], enter_ref[level], NT)
        states = base_ref[level] + dot3(corner, entry_ref[level], NN)
        coefs = jnp.broadcast_to(coef_ref[level:level + 1, :], (8, N))
        out_ref[2 * level] = jnp.where(left, states, coefs)
        out_ref[2 * level + 1] = jnp.where(left, pltpu.roll(states, HALF, 1), coefs)


def apply_y_kernel(states_ref, out_ref, spread, links):
    blocks = states_ref.shape[0]
    coefs = states_ref[:, 0, :]
    for m in range(4 + len(COEFS)):
        spread[m] = jnp.broadcast_to(coefs[:, HALF + m:HALF + m + 1], (blocks, N))
    run_links(
        blocks,
        lambda j, k: states_ref[j, k:k + 1, :],
        spread,
        lambda j, k, value: links.__setitem__((j, slice(k, k + 1), slice(None)), value),
    )
    left = lanes((4, N)) < HALF
    for j in range(blocks):
        out_ref[j] = jnp.where(left, links[j, 0:4, :], pltpu.roll(links[j, 4:8, :], HALF, 1))


def local_y_kernel(base_ref, enter_ref, entry_ref, filter_ref, out_ref):
    for level in range(out_ref.shape[0]):
        rows = base_ref[level] + dot3(enter_ref[level], entry_ref[level], TN)
        out_ref[level] = dot3(filter_ref[level], rows, NN)


def vertical_kernel(taps_ref, values_ref, out_ref):
    levels = out_ref.shape[0]
    for level in range(levels):
        total = None
        for d in range(5):
            other = level + d - 2
            if 0 <= other < levels:
                term = taps_ref[d, level] * values_ref[other]
                total = term if total is None else total + term
        out_ref[level] = total


def final_kernel(taps_ref, values_ref, slots_ref, entry_ref, out_ref, enter):
    levels = out_ref.shape[0]
    left = lanes((4, N)) < HALF
    for level in range(levels):
        a, b = slots_ref[2 * level], slots_ref[2 * level + 1]
        enter[level, 0:4, :] = jnp.where(left, a, pltpu.roll(b, HALF, 1))
        enter[level, 4:8, :] = jnp.where(left, pltpu.roll(a, HALF, 1), b)
    for level in range(levels):
        weights, states = [], []
        for d in range(5):
            other = level + d - 2
            if 0 <= other < levels:
                weights.append(taps_ref[d, level] * entry_ref[other])
                states.append(enter[other])
        weights = jnp.concatenate(weights, 0)
        states = jnp.concatenate(states, 0)
        out_ref[level] = values_ref[level] + dot3(weights, states, TN)


VM = pl.BlockSpec(memory_space=pltpu.VMEM)
SM = pl.BlockSpec(memory_space=pltpu.SMEM)


def call(kernel, shapes, args, scratch=(), flops=0, smem=()):
    outs = [jax.ShapeDtypeStruct(shape, F32) for shape in shapes]
    moved = 4 * sum(x.size for x in list(args) + outs)
    result = pl.pallas_call(
        kernel,
        out_shape=outs if len(outs) > 1 else outs[0],
        in_specs=[SM if k in smem else VM for k in range(len(args))],
        out_specs=[VM] * len(outs) if len(outs) > 1 else VM,
        scratch_shapes=[pltpu.VMEM(shape, F32) for shape in scratch],
        compiler_params=pltpu.CompilerParams(vmem_limit_bytes=GRANT),
        cost_estimate=pl.CostEstimate(flops=flops, bytes_accessed=moved, transcendentals=0),
    )(*args)
    return result


def exchange(value, axis):
    return lax.all_to_all(value, axis, 0, 0, tiled=True)


def steps(control, scale_x, scale_y, taps):
    levels = control.shape[0]
    full, small = (levels, N, N), (levels, 8, N)
    nx, ny = lax.axis_size("gx"), lax.axis_size("gy")
    table = (N, levels, N)
    bind = functools.partial

    closing = call(states_x_kernel, [small], (scale_x, control), [small])
    closing = exchange(closing, "gx")
    link = call(link_x_kernel, [(8 * nx, N)], (scale_x,), [(nx, N), (14, nx, N)])
    filter_x = call(bind(filter_kernel, "gx"), [full], (scale_x,), [table, table])

    enter_x = call(apply_x_kernel, [small], (link, closing))
    enter_x = exchange(enter_x, "gx")
    entry_x, gain_x, extract_y, entry_y, coefs = call(
        tables_kernel, [small, (levels, N), small, small, (levels, N)], (scale_x, scale_y)
    )
    local, base = call(local_x_kernel, [full, small], (control, gain_x, filter_x, extract_y))

    slots = call(states_y_kernel, [(ny, 8, N)], (enter_x, entry_x, extract_y, base, coefs))
    slots = exchange(slots, "gy")
    filter_y = call(bind(filter_kernel, None), [full], (scale_y,), [table, table])
    local = call(local_y_kernel, [full], (local, enter_x, entry_x, filter_y))

    slots = call(apply_y_kernel, [(ny, 4, N)], (slots,), [(14, ny, N), (ny, 8, N)])
    slots = exchange(slots, "gy")
    local = call(vertical_kernel, [full], (taps, local), smem=(0,))
    return call(final_kernel, [full], (taps, local, slots, entry_y), [small], smem=(0,))


def solution(mesh):
    return jax.shard_map(
        steps,
        mesh=mesh,
        in_specs=(P(None, "gy", "gx"), P(), P(None, "gy"), P()),
        out_specs=P(None, "gy", "gx"),
        check_vma=False,
    )
```

```python
import functools
import jax
import jax.numpy as jnp
from jax import lax
from jax.experimental import pallas as pl
from jax.experimental.pallas import tpu as pltpu
from jax.sharding import PartitionSpec as P


F32 = jnp.float32
BF16 = jnp.bfloat16
N = 128
HALF = 64
GRANT = 16 << 20
CHUNK = 4
SENT = 8


def split(a):
    high = a.astype(BF16)
    return high, (a - high.astype(F32)).astype(BF16)


def dot3(a, b, dims):
    ah, al = a if isinstance(a, tuple) else split(a)
    bh, bl = b if isinstance(b, tuple) else split(b)

    def one(u, v):
        return lax.dot_general(u, v, (dims, ((), ())), preferred_element_type=F32)

    return one(ah, bh) + (one(ah, bl) + one(al, bh))


def wide_left(a):
    return jnp.concatenate(split(a), 1)


def wide_right(b):
    high, low = split(b)
    top = jnp.concatenate([high, low], 1)
    return jnp.concatenate([top, jnp.concatenate([high, jnp.zeros_like(low)], 1)], 0)


def wide_dot(left, right):
    both = lax.dot_general(left, right, (NN, ((), ())), preferred_element_type=F32)
    return both[:, :N] + both[:, N:]


NN = ((1,), (0,))
NT = ((1,), (1,))
TN = ((0,), (0,))


def poly(a, b):
    out = []
    for k in range(4):
        total = a[0] * b[k]
        for m in range(1, k + 1):
            total = total + a[m] * b[k - m]
        out.append(total)
    return out


def geometric(lead, q):
    out = [lead]
    for _ in range(3):
        out.append(out[-1] * q)
    return out


def sym(table, a, b):
    return table[(max(a, b), min(a, b))]


def congruence(t, r):
    x = {}
    for c in range(4):
        for a in range(4):
            total = t[0] * sym(r, a, c)
            for m in range(1, a + 1):
                total = total + t[m] * sym(r, a - m, c)
            x[(a, c)] = total
    out = {}
    for a in range(4):
        for b in range(a + 1):
            total = t[0] * x[(a, b)]
            for m in range(1, b + 1):
                total = total + t[m] * x[(a, b - m)]
            out[(a, b)] = total
    return out


def lanes(shape):
    return lax.broadcasted_iota(jnp.int32, shape, len(shape) - 1)


def later(x, d, fill):
    moved = pltpu.roll(x, N - d, 1)
    return jnp.where(lanes(x.shape) < N - d, moved, fill)


def earlier(x, d, fill):
    moved = pltpu.roll(x, d, 1)
    return jnp.where(lanes(x.shape) >= d, moved, fill)


def ones_first(k):
    return 1.0 if k == 0 else 0.0


def poles(scale):
    p = jnp.exp(-1.0 / scale)
    return p, 1.0 - p


def suffix_scan(p, q):
    t = geometric(p, q)
    g = [p * q]
    for _ in range(6):
        g.append(g[-1] * q)
    r = {(a, b): g[a + b] for a in range(4) for b in range(a + 1)}
    d = 1
    while d < N:
        t2 = [later(t[k], d, ones_first(k)) for k in range(4)]
        r2 = {key: later(value, d, 0.0) for key, value in r.items()}
        grown = congruence(t, r2)
        r = {key: r[key] + grown[key] for key in r}
        t = poly(t, t2)
        d *= 2
    return t, r


def prefix_scan(p, q):
    t = geometric(p, q)
    d = 1
    while d < N:
        t = poly(t, [earlier(t[k], d, ones_first(k)) for k in range(4)])
        d *= 2
    return t


def return_map(r, s):
    out = []
    for a in range(4):
        total = sym(r, a, 3) * s[0]
        for b in range(1, 4):
            total = total + sym(r, a, 3 - b) * s[b]
        out.append(total)
    return out


def extraction(p, q, t, r, before):
    inject = geometric(q, q)
    t_next = [later(t[k], 1, ones_first(k)) for k in range(4)]
    r_next = {key: later(value, 1, 0.0) for key, value in r.items()}
    f = poly(t_next, inject)
    back = poly(geometric(p, q), return_map(r_next, inject))
    back = [back[k] + inject[k] * inject[3] for k in range(4)]
    px = [earlier(before[k], 1, ones_first(k)) for k in range(4)]
    return f, poly(px, back)


def response(t, r, before):
    px = [earlier(before[k], 1, ones_first(k)) for k in range(4)]
    out = []
    for k in range(4):
        total = sym(r, 3, 3 - k) * px[0]
        for b in range(k + 1, 4):
            total = total + sym(r, 3, 3 - b) * px[b - k]
        out.append(total)
    return out + [t[3 - k] for k in range(4)]


COEFS = [(a, b) for a in range(4) for b in range(a + 1)]


def own_scale(axis, scale_ref):
    if axis is None:
        return scale_ref[...]
    me = lax.axis_index(axis)
    return scale_ref[:, pl.ds(pl.multiple_of(me * N, N), N)]


def flat(value):
    return value.reshape(value.shape[0] * value.shape[1], value.shape[2])


def states_x_kernel(scale_hbm, control_hbm, out_ref, scale_ref, control_ref, weights, sems):
    levels = out_ref.shape[0]
    me = lax.axis_index("gx")
    first = pltpu.make_async_copy(
        scale_hbm.at[:, pl.ds(pl.multiple_of(me * N, N), N)], scale_ref, sems.at[0]
    )
    second = pltpu.make_async_copy(control_hbm, control_ref, sems.at[1])
    first.start()
    second.start()
    first.wait()
    scale = scale_ref[...]
    p, q = poles(scale)
    t, r = suffix_scan(p, q)
    before = prefix_scan(p, q)
    f, b = extraction(p, q, t, r, before)
    amplitude = jnp.sqrt(8.0 * scale)
    for k in range(4):
        weights[pl.ds(k, levels, stride=8), :] = f[k] * amplitude
        weights[pl.ds(4 + k, levels, stride=8), :] = b[k] * amplitude
    right = wide_right(weights[...].T)
    owner = lanes((N, N)) // 8
    total = jnp.zeros((N, N), F32)
    second.wait()
    for level in range(0, levels, CHUNK):
        every = wide_dot(wide_left(flat(control_ref[level:level + CHUNK])), right)
        for k in range(CHUNK):
            total = jnp.where(owner == level + k, every[k * N:(k + 1) * N], total)
    out_ref[...] = total.T.reshape(levels, 8, N)


def link_x_kernel(scale_ref, out_ref, gathered, spread):
    blocks = out_ref.shape[0] // 8
    me = lax.axis_index("gx")
    level = lax.broadcasted_iota(jnp.int32, (scale_ref.shape[0], N), 0)
    for j in range(blocks):
        block = jnp.where(level == me, scale_ref[:, j * N:(j + 1) * N], 0.0)
        gathered[j:j + 1, :] = jnp.sum(block, axis=0, keepdims=True)
    p, q = poles(gathered[...])
    t, r = suffix_scan(p, q)
    for k in range(4):
        spread[k] = jnp.broadcast_to(t[k][:, 0:1], (blocks, N))
    for m, key in enumerate(COEFS):
        spread[4 + m] = jnp.broadcast_to(r[key][:, 0:1], (blocks, N))
    lane = lanes((1, N))
    run_links(
        blocks,
        lambda j, k: (lane == 8 * j + k).astype(F32),
        spread,
        lambda j, k, value: out_ref.__setitem__((pl.ds(8 * j + k, 1), slice(None)), value),
    )


def run_links(blocks, source, spread, store):
    zero = jnp.zeros((1, N), F32)
    s = [zero] * 4
    returns = []
    for j in range(blocks):
        t = [spread[k, j:j + 1, :] for k in range(4)]
        r = {key: spread[4 + m, j:j + 1, :] for m, key in enumerate(COEFS)}
        for k in range(4):
            store(j, k, s[k])
        back = return_map(r, s)
        returns.append([back[k] + source(j, 4 + k) for k in range(4)])
        moved = poly(t, s)
        s = [moved[k] + source(j, k) for k in range(4)]
    e = [zero] * 4
    for j in reversed(range(blocks)):
        t = [spread[k, j:j + 1, :] for k in range(4)]
        for k in range(4):
            store(j, 4 + k, e[k])
        moved = poly(t, e)
        e = [moved[k] + returns[j][k] for k in range(4)]


def apply_x_kernel(link_ref, states_ref, out_ref):
    blocks = out_ref.shape[0]
    flat = states_ref[...].reshape(blocks * 8, N)
    out_ref[...] = dot3(link_ref[...], flat, NN).reshape(blocks, 8, N)


def filter_kernel(axis, scale_ref, local_ref, spread, middle):
    scale = own_scale(axis, scale_ref)
    levels = scale.shape[0]
    p, q = poles(scale)
    for i in range(N):
        spread[i] = jnp.broadcast_to(p[:, i:i + 1], (levels, N))
    shape = (levels, N)
    lane = lanes(shape)
    zero = jnp.zeros(shape, F32)
    column = jnp.sqrt(8.0 * scale) if axis is None else p / q

    def advance(factor, state, inflow):
        rest = 1.0 - factor
        out = []
        for k in range(4):
            inflow = factor * state[k] + rest * inflow
            out.append(inflow)
        return out

    def forward(i, state):
        state = advance(spread[i], state, (lane == i).astype(F32))
        middle[i] = state[3]
        return tuple(state)

    lax.fori_loop(0, N, forward, (zero,) * 4, unroll=8)

    def backward(k, state):
        i = N - 1 - k
        state = advance(spread[i], state, middle[i])
        local_ref[:, pl.ds(i, 1), :] = (state[3] * column).reshape(levels, 1, N)
        return tuple(state)

    lax.fori_loop(0, N, backward, (zero,) * 4, unroll=8)


def tables_kernel(scale_x_ref, scale_y_ref, entry_x_ref, gain_x_ref, extract_ref, entry_y_ref, coef_ref):
    levels = scale_y_ref.shape[0]
    scale = jnp.concatenate([own_scale("gx", scale_x_ref), scale_y_ref[...]], 0)
    p, q = poles(scale)
    t, r = suffix_scan(p, q)
    before = prefix_scan(p, q)
    amplitude = jnp.sqrt(8.0 * scale)
    gain_x_ref[...] = (amplitude * q / p)[:levels]
    for k, row in enumerate(response(t, r, before)):
        entry_x_ref[:, k, :] = row[:levels]
        entry_y_ref[:, k, :] = row[levels:]
    p, q, amplitude = p[levels:], q[levels:], amplitude[levels:]
    t = [value[levels:] for value in t]
    r = {key: value[levels:] for key, value in r.items()}
    f, b = extraction(p, q, t, r, [value[levels:] for value in before])
    for k in range(4):
        extract_ref[:, k, :] = f[k] * amplitude
        extract_ref[:, 4 + k, :] = b[k] * amplitude
    shape = p.shape
    lane = lanes(shape)
    coefs = jnp.zeros(shape, F32)
    for m, value in enumerate(t + [r[key] for key in COEFS]):
        coefs = jnp.where(lane == HALF + m, jnp.broadcast_to(value[:, 0:1], shape), coefs)
    coef_ref[...] = coefs


def local_x_kernel(control_ref, gain_ref, filter_ref, extract_ref, out_ref, base_ref):
    for level in range(out_ref.shape[0]):
        g = dot3(control_ref[level] * gain_ref[level:level + 1, :], filter_ref[level], NN)
        out_ref[level] = g
        base_ref[level] = dot3(extract_ref[level], g, NN)


def states_y_kernel(enter_ref, entry_ref, extract_ref, base_ref, coef_ref, out_ref):
    levels = base_ref.shape[0]
    corner = dot3(flat(extract_ref[...]), flat(enter_ref[...]), NT)
    here = lax.broadcasted_iota(jnp.int32, (N, N), 0) // 8 == lanes((N, N)) // 8
    corner = jnp.where(here, corner, 0.0)
    states = flat(base_ref[...]) + dot3(corner, flat(entry_ref[...]), NN)
    left = lanes((8, N)) < HALF
    for level in range(levels):
        own = states[8 * level:8 * level + 8]
        coefs = jnp.broadcast_to(coef_ref[level:level + 1, :], (8, N))
        out_ref[2 * level] = jnp.where(left, own, coefs)
        out_ref[2 * level + 1] = jnp.where(left, pltpu.roll(own, HALF, 1), coefs)


def run_groups(groups, size, reverse, maps, source, store, ends, starts):
    steps = range(size - 1, -1, -1) if reverse else range(size)
    total, state, kept = None, None, []
    for j in steps:
        kept.append((j, total, state))
        t, f = maps(j), source(j)
        state = f if state is None else [a + b for a, b in zip(poly(t, state), f)]
        total = t if total is None else poly(t, total)
    for k in range(4):
        ends[k], ends[4 + k] = total[k], state[k]
    enter = [jnp.zeros((1, N), F32)] * 4
    for c in range(groups - 1, -1, -1) if reverse else range(groups):
        row = slice(c, c + 1)
        for k in range(4):
            starts[k, row, :] = enter[k]
        moved = poly([ends[k, row, :] for k in range(4)], enter)
        enter = [moved[k] + ends[4 + k, row, :] for k in range(4)]
    enter = [starts[k] for k in range(4)]
    for j, total, state in kept:
        store(j, enter if total is None else [a + b for a, b in zip(poly(total, enter), state)])


def apply_y_kernel(states_ref, out_ref, packed, spread, links, returns, ends, starts):
    blocks = states_ref.shape[0] // 8
    groups = ends.shape[1]
    size = blocks // groups
    packed[...] = states_ref[pl.ds(0, blocks, stride=8), :]

    def coef(m):
        return jnp.broadcast_to(packed[:, HALF + m:HALF + m + 1], (blocks, N))

    for m in range(4):
        spread[m] = coef(m)

    def rows(j):
        return pl.ds(j, groups, stride=size)

    def store(first):
        def put(j, values):
            for k in range(4):
                links[first + k, rows(j), :] = values[k]

        return put

    def maps(j):
        return [spread[k, rows(j), :] for k in range(4)]

    for k in range(4):
        returns[k] = states_ref[pl.ds(k, blocks, stride=8), :]

    def source(j):
        return [returns[k, rows(j), :] for k in range(4)]

    run_groups(groups, size, False, maps, source, store(0), ends, starts)
    r = {key: coef(4 + m) for m, key in enumerate(COEFS)}
    back = return_map(r, [links[k] for k in range(4)])
    for k in range(4):
        returns[k] = back[k] + states_ref[pl.ds(4 + k, blocks, stride=8), :]
    run_groups(groups, size, True, maps, source, store(4), ends, starts)
    left = lanes((blocks, N)) < HALF
    for k in range(4):
        out_ref[pl.ds(k, blocks, stride=4), :] = jnp.where(
            left, links[k], pltpu.roll(links[4 + k], HALF, 1)
        )


def local_y_kernel(base_ref, enter_ref, entry_ref, filter_ref, out_ref):
    for level in range(out_ref.shape[0]):
        rows = base_ref[level] + dot3(enter_ref[level], entry_ref[level], TN)
        out_ref[level] = dot3(filter_ref[level], rows, NN)


def vertical_kernel(taps_ref, values_ref, entry_ref, out_ref, wide_ref):
    levels = out_ref.shape[0]
    turned = flat(entry_ref[...]).T
    owner = lanes((1, N)) // 8
    for level in range(levels):
        total, row = None, jnp.zeros((1, N), F32)
        for d in range(5):
            other = level + d - 2
            if 0 <= other < levels:
                term = taps_ref[d, level] * values_ref[other]
                total = term if total is None else total + term
                row = jnp.where(owner == other, taps_ref[d, level], row)
        out_ref[level] = total
        wide_ref[level] = wide_left(turned * row)


def final_kernel(values_ref, wide_ref, slots_ref, out_hbm, enter, whole, sems):
    levels = enter.shape[0]
    left = lanes((4, N)) < HALF
    for level in range(levels):
        a, b = slots_ref[2 * level], slots_ref[2 * level + 1]
        enter[level, 0:4, :] = jnp.where(left, a, pltpu.roll(b, HALF, 1))
        enter[level, 4:8, :] = jnp.where(left, pltpu.roll(a, HALF, 1), b)
    right = wide_right(flat(enter[...]))
    copies = []
    for level in range(0, levels, CHUNK):
        part = pl.ds(level, CHUNK)
        added = wide_dot(flat(wide_ref[part]), right).reshape(CHUNK, N, N)
        whole[part] = values_ref[part] + added
        if (level + CHUNK) % SENT == 0:
            part = pl.ds(level + CHUNK - SENT, SENT)
            copies.append(
                pltpu.make_async_copy(whole.at[part], out_hbm.at[part], sems.at[level // SENT])
            )
            copies[-1].start()
    for copy in copies:
        copy.wait()


VM = pl.BlockSpec(memory_space=pltpu.VMEM)
SM = pl.BlockSpec(memory_space=pltpu.SMEM)
HB = pl.BlockSpec(memory_space=pltpu.HBM)


def call(kernel, shapes, args, scratch=(), ins=None, out=VM, sems=0, types=None, grant=GRANT):
    types = types or [F32] * len(shapes)
    outs = [jax.ShapeDtypeStruct(shape, dtype) for shape, dtype in zip(shapes, types)]
    moved = 4 * sum(x.size for x in list(args) + outs)
    scratch = [pltpu.VMEM(shape, F32) for shape in scratch]
    if sems:
        scratch.append(pltpu.SemaphoreType.DMA((sems,)))
    return pl.pallas_call(
        kernel,
        out_shape=outs if len(outs) > 1 else outs[0],
        in_specs=ins or [VM] * len(args),
        out_specs=[out] * len(outs) if len(outs) > 1 else out,
        scratch_shapes=scratch,
        compiler_params=pltpu.CompilerParams(vmem_limit_bytes=grant),
        cost_estimate=pl.CostEstimate(flops=0, bytes_accessed=moved, transcendentals=0),
    )(*args)


def exchange(value, axis):
    return lax.all_to_all(value, axis, 0, 0, tiled=True)


def steps(control, scale_x, scale_y, taps):
    levels = control.shape[0]
    full, small = (levels, N, N), (levels, 8, N)
    nx, ny = lax.axis_size("gx"), lax.axis_size("gy")
    table = (N, levels, N)
    bind = functools.partial

    closing = call(
        states_x_kernel,
        [small],
        (scale_x, control),
        [(levels, N), full, (8 * levels, N)],
        ins=[HB, HB],
        sems=2,
        grant=60 << 20,
    )
    closing = exchange(closing, "gx")
    link = call(link_x_kernel, [(8 * nx, N)], (scale_x,), [(nx, N), (14, nx, N)])
    filter_x = call(bind(filter_kernel, "gx"), [full], (scale_x,), [table, table])

    enter_x = call(apply_x_kernel, [small], (link, closing))
    enter_x = exchange(enter_x, "gx")
    entry_x, gain_x, extract_y, entry_y, coefs = call(
        tables_kernel, [small, (levels, N), small, small, (levels, N)], (scale_x, scale_y)
    )
    local, base = call(local_x_kernel, [full, small], (control, gain_x, filter_x, extract_y))

    slots = call(states_y_kernel, [(ny, 8, N)], (enter_x, entry_x, extract_y, base, coefs))
    slots = exchange(slots, "gy")
    filter_y = call(bind(filter_kernel, None), [full], (scale_y,), [table, table])
    local = call(local_y_kernel, [full], (local, enter_x, entry_x, filter_y))

    slots = call(
        apply_y_kernel,
        [(4 * ny, N)],
        (slots.reshape(8 * ny, N),),
        [(ny, N), (4, ny, N), (8, ny, N), (4, ny, N), (8, 8, N), (4, 8, N)],
    )
    slots = exchange(slots.reshape(ny, 4, N), "gy")
    local, wide = call(
        vertical_kernel,
        [full, (levels, N, 2 * N)],
        (taps, local, entry_y),
        ins=[SM, VM, VM],
        types=[F32, BF16],
    )
    return call(
        final_kernel, [full], (local, wide, slots), [small, full], out=HB, sems=levels // SENT
    )


def solution(mesh):
    return jax.shard_map(
        steps,
        mesh=mesh,
        in_specs=(P(None, "gy", "gx"), P(), P(None, "gy"), P()),
        out_specs=P(None, "gy", "gx"),
        check_vma=False,
    )
```

```python
import functools
import jax
import jax.numpy as jnp
from jax import lax
from jax.experimental import pallas as pl
from jax.experimental.pallas import tpu as pltpu
from jax.sharding import PartitionSpec as P


F32 = jnp.float32
BF16 = jnp.bfloat16
N = 128
HALF = 64
GRANT = 16 << 20
CHUNK = 4
SENT = 8


def split(a):
    high = a.astype(BF16)
    return high, (a - high.astype(F32)).astype(BF16)


def dot3(a, b, dims):
    ah, al = a if isinstance(a, tuple) else split(a)
    bh, bl = b if isinstance(b, tuple) else split(b)

    def one(u, v):
        return lax.dot_general(u, v, (dims, ((), ())), preferred_element_type=F32)

    return one(ah, bh) + (one(ah, bl) + one(al, bh))


def wide_left(a):
    return jnp.concatenate(split(a), 1)


def wide_right(b):
    high, low = split(b)
    top = jnp.concatenate([high, low], 1)
    return jnp.concatenate([top, jnp.concatenate([high, jnp.zeros_like(low)], 1)], 0)


def wide_dot(left, right):
    both = lax.dot_general(left, right, (NN, ((), ())), preferred_element_type=F32)
    return both[:, :N] + both[:, N:]


NN = ((1,), (0,))
NT = ((1,), (1,))
TN = ((0,), (0,))


def poly(a, b):
    out = []
    for k in range(4):
        total = a[0] * b[k]
        for m in range(1, k + 1):
            total = total + a[m] * b[k - m]
        out.append(total)
    return out


def geometric(lead, q):
    out = [lead]
    for _ in range(3):
        out.append(out[-1] * q)
    return out


def sym(table, a, b):
    return table[(max(a, b), min(a, b))]


def congruence(t, r):
    x = {}
    for c in range(4):
        for a in range(4):
            total = t[0] * sym(r, a, c)
            for m in range(1, a + 1):
                total = total + t[m] * sym(r, a - m, c)
            x[(a, c)] = total
    out = {}
    for a in range(4):
        for b in range(a + 1):
            total = t[0] * x[(a, b)]
            for m in range(1, b + 1):
                total = total + t[m] * x[(a, b - m)]
            out[(a, b)] = total
    return out


def lanes(shape):
    return lax.broadcasted_iota(jnp.int32, shape, len(shape) - 1)


def later(x, d, fill):
    moved = pltpu.roll(x, N - d, 1)
    return jnp.where(lanes(x.shape) < N - d, moved, fill)


def earlier(x, d, fill):
    moved = pltpu.roll(x, d, 1)
    return jnp.where(lanes(x.shape) >= d, moved, fill)


def ones_first(k):
    return 1.0 if k == 0 else 0.0


def poles(scale):
    p = jnp.exp(-1.0 / scale)
    return p, 1.0 - p


def suffix_scan(p, q):
    t = geometric(p, q)
    g = [p * q]
    for _ in range(6):
        g.append(g[-1] * q)
    r = {(a, b): g[a + b] for a in range(4) for b in range(a + 1)}
    d = 1
    while d < N:
        t2 = [later(t[k], d, ones_first(k)) for k in range(4)]
        r2 = {key: later(value, d, 0.0) for key, value in r.items()}
        grown = congruence(t, r2)
        r = {key: r[key] + grown[key] for key in r}
        t = poly(t, t2)
        d *= 2
    return t, r


def prefix_scan(p, q):
    t = geometric(p, q)
    d = 1
    while d < N:
        t = poly(t, [earlier(t[k], d, ones_first(k)) for k in range(4)])
        d *= 2
    return t


def return_map(r, s):
    out = []
    for a in range(4):
        total = sym(r, a, 3) * s[0]
        for b in range(1, 4):
            total = total + sym(r, a, 3 - b) * s[b]
        out.append(total)
    return out


def extraction(p, q, t, r, before):
    inject = geometric(q, q)
    t_next = [later(t[k], 1, ones_first(k)) for k in range(4)]
    r_next = {key: later(value, 1, 0.0) for key, value in r.items()}
    f = poly(t_next, inject)
    back = poly(geometric(p, q), return_map(r_next, inject))
    back = [back[k] + inject[k] * inject[3] for k in range(4)]
    px = [earlier(before[k], 1, ones_first(k)) for k in range(4)]
    return f, poly(px, back)


def response(t, r, before):
    px = [earlier(before[k], 1, ones_first(k)) for k in range(4)]
    out = []
    for k in range(4):
        total = sym(r, 3, 3 - k) * px[0]
        for b in range(k + 1, 4):
            total = total + sym(r, 3, 3 - b) * px[b - k]
        out.append(total)
    return out + [t[3 - k] for k in range(4)]


COEFS = [(a, b) for a in range(4) for b in range(a + 1)]


def own_scale(axis, scale_ref):
    if axis is None:
        return scale_ref[...]
    me = lax.axis_index(axis)
    return scale_ref[:, pl.ds(pl.multiple_of(me * N, N), N)]


def flat(value):
    return value.reshape(value.shape[0] * value.shape[1], value.shape[2])


def combine(first, second):
    t, r = first
    grown = congruence(t, second[1])
    return poly(t, second[0]), {key: r[key] + grown[key] for key in r}


def block_maps(scale_ref, table):
    levels = scale_ref.shape[0]
    per = N // levels
    out = []
    for h in range(scale_ref.shape[1] // (per * N)):
        rows = [scale_ref[:, (h * per + j) * N:(h * per + j + 1) * N] for j in range(per)]
        turned = jnp.concatenate(rows, 0).T
        table[h] = jnp.exp(-1.0 / turned)
        t, r = None, None
        for i in range(N // 8):
            p = table[h, pl.ds(i, 8, stride=N // 8), :]
            q = 1.0 - p
            if t is None:
                t = geometric(p, q)
            else:
                t = [p * value for value in t]
                for k in range(1, 4):
                    t[k] = t[k] + q * t[k - 1]
            lead = [q / p * value for value in t]
            grown = {key: lead[key[0]] * t[key[1]] for key in COEFS}
            r = grown if r is None else {key: r[key] + grown[key] for key in COEFS}
        for d in (1, 2, 4):
            move = functools.partial(pltpu.roll, shift=8 - d, axis=0)
            t, r = combine((t, r), ([move(v) for v in t], {key: move(v) for key, v in r.items()}))
        out.append(([v[0:1] for v in t], {key: v[0:1] for key, v in r.items()}))
    return out


def return_after(maps, me, levels):
    per = N // levels
    block = lanes((1, N)) // levels
    halves = []
    for h, (t, r) in enumerate(maps):
        after = block + h * per > me
        t = [jnp.where(after, t[k], ones_first(k)) for k in range(4)]
        r = {key: jnp.where(after, v, 0.0) for key, v in r.items()}
        for d in (1, 2, 4):
            move = functools.partial(pltpu.roll, shift=N - levels * d, axis=1)
            t, r = combine((t, r), ([move(v) for v in t], {key: move(v) for key, v in r.items()}))
        halves.append((t, r))
    r = combine(halves[0], halves[1])[1]
    rows = [r[key] for key in COEFS]
    rows = jnp.concatenate(rows + [rows[0]] * (16 - len(rows)), 0).T
    return {
        key: jnp.broadcast_to(rows[:levels, m:m + 1], (levels, N)) for m, key in enumerate(COEFS)
    }


def states_x_kernel(scale_hbm, control_hbm, out_ref, scale_ref, control_ref, weights, table, sems):
    levels = scale_ref.shape[0]
    blocks = out_ref.shape[0]
    me = lax.axis_index("gx")
    first = pltpu.make_async_copy(scale_hbm, scale_ref, sems.at[0])
    second = pltpu.make_async_copy(control_hbm, control_ref, sems.at[1])
    first.start()
    second.start()
    first.wait()
    back_map = return_after(block_maps(scale_ref, table), me, levels)
    scale = own_scale("gx", scale_ref)
    p, q = poles(scale)
    t, r = suffix_scan(p, q)
    before = prefix_scan(p, q)
    f, b = extraction(p, q, t, r, before)
    own = [jnp.broadcast_to(t[k][:, 0:1], (levels, N)) for k in range(4)]
    returned = poly(own, return_map(back_map, f))
    b = [b[k] + returned[k] for k in range(4)]
    amplitude = jnp.sqrt(8.0 * scale)
    for k in range(4):
        weights[pl.ds(k, levels, stride=4), :] = f[k] * amplitude
        weights[pl.ds(4 * levels + k, levels, stride=4), :] = b[k] * amplitude
    right = wide_right(weights[...].T)
    owner = (lanes((N, N)) % (4 * levels)) // 4
    total = jnp.zeros((N, N), F32)
    second.wait()
    for level in range(0, levels, CHUNK):
        every = wide_dot(wide_left(flat(control_ref[level:level + CHUNK])), right)
        for k in range(CHUNK):
            total = jnp.where(owner == level + k, every[k * N:(k + 1) * N], total)
    weights[...] = total.T
    for j in range(blocks):
        start = pl.multiple_of(jnp.where(me > j, 4 * levels, 0), 4 * levels)
        out_ref[j] = weights[pl.ds(start, 4 * levels), :]


def links_x_kernel(scale_ref, link_ref, table):
    levels = scale_ref.shape[0]
    blocks = scale_ref.shape[1] // N
    per = N // levels
    me = lax.axis_index("gx")
    maps = block_maps(scale_ref, table)
    back_map = return_after(maps, me, levels)
    for m, key in enumerate(COEFS):
        link_ref[4 * blocks + 4 + m] = back_map[key]
    rows = [t[k] for t, _ in maps for k in range(4)]
    turned = jnp.concatenate(rows, 0).T

    def block(j):
        h, i = j // per, j % per
        part = turned[i * levels:(i + 1) * levels]
        return [
            jnp.broadcast_to(part[:, 4 * h + k:4 * h + k + 1], (levels, N)) for k in range(4)
        ]

    unit = [jnp.full((levels, N), ones_first(k), F32) for k in range(4)]
    own = [jnp.zeros((levels, N), F32)] * 4
    current = unit
    for j in reversed(range(blocks)):
        t = block(j)
        for k in range(4):
            link_ref[4 * j + k] = jnp.where(me > j, current[k], 0.0)
        moved = poly(t, current)
        current = [jnp.where(me > j, moved[k], unit[k]) for k in range(4)]
        own = [jnp.where(me == j, t[k], own[k]) for k in range(4)]
    current = unit
    for j in range(blocks):
        t = block(j)
        for k in range(4):
            link_ref[4 * j + k] = link_ref[4 * j + k] + jnp.where(me < j, current[k], 0.0)
        moved = poly(t, current)
        current = [jnp.where(me < j, moved[k], unit[k]) for k in range(4)]
    for k in range(4):
        link_ref[4 * blocks + k] = own[k]


def filter_kernel(axis, scale_ref, local_ref, spread, middle):
    scale = own_scale(axis, scale_ref)
    levels = scale.shape[0]
    p, q = poles(scale)
    for i in range(N):
        spread[i] = jnp.broadcast_to(p[:, i:i + 1], (levels, N))
    shape = (levels, N)
    lane = lanes(shape)
    zero = jnp.zeros(shape, F32)
    column = jnp.sqrt(8.0 * scale) if axis is None else p / q

    def advance(factor, state, inflow):
        rest = 1.0 - factor
        out = []
        for k in range(4):
            inflow = factor * state[k] + rest * inflow
            out.append(inflow)
        return out

    def forward(i, state):
        state = advance(spread[i], state, (lane == i).astype(F32))
        middle[i] = state[3]
        return tuple(state)

    lax.fori_loop(0, N, forward, (zero,) * 4, unroll=16)

    def backward(k, state):
        i = N - 1 - k
        state = advance(spread[i], state, middle[i])
        local_ref[pl.ds(i, levels, stride=N), :] = state[3] * column
        return tuple(state)

    lax.fori_loop(0, N, backward, (zero,) * 4, unroll=16)


def tables_kernel(scale_x_ref, scale_y_ref, entry_x_ref, gain_x_ref, extract_ref, entry_y_ref, coef_ref):
    levels = scale_y_ref.shape[0]
    scale = jnp.concatenate([own_scale("gx", scale_x_ref), scale_y_ref[...]], 0)
    p, q = poles(scale)
    t, r = suffix_scan(p, q)
    before = prefix_scan(p, q)
    amplitude = jnp.sqrt(8.0 * scale)
    gain_x_ref[...] = (amplitude * q / p)[:levels]
    for k, row in enumerate(response(t, r, before)):
        entry_x_ref[:, k, :] = row[:levels]
        entry_y_ref[:, k, :] = row[levels:]
    p, q, amplitude = p[levels:], q[levels:], amplitude[levels:]
    t = [value[levels:] for value in t]
    r = {key: value[levels:] for key, value in r.items()}
    f, b = extraction(p, q, t, r, [value[levels:] for value in before])
    for k in range(4):
        extract_ref[:, k, :] = f[k] * amplitude
        extract_ref[:, 4 + k, :] = b[k] * amplitude
    shape = p.shape
    lane = lanes(shape)
    coefs = jnp.zeros(shape, F32)
    for m, value in enumerate(t + [r[key] for key in COEFS]):
        coefs = jnp.where(lane == HALF + m, jnp.broadcast_to(value[:, 0:1], shape), coefs)
    coef_ref[...] = coefs


def local_x_kernel(control_ref, gain_ref, filter_ref, extract_ref, out_ref, base_ref):
    for level in range(out_ref.shape[0]):
        g = dot3(control_ref[level] * gain_ref[level:level + 1, :], filter_ref[level], NN)
        out_ref[level] = g
        base_ref[level] = dot3(extract_ref[level], g, NN)


def states_y_kernel(
    sent_ref, link_ref, entry_ref, extract_ref, base_ref, coef_ref, out_ref, enter_ref
):
    levels = base_ref.shape[0]
    blocks = sent_ref.shape[0] // (4 * levels)
    me = lax.axis_index("gx")
    zero = jnp.zeros((levels, N), F32)
    s, e = [zero] * 4, [zero] * 4
    for j in range(blocks):
        sent = [sent_ref[pl.ds(4 * levels * j + k, levels, stride=4), :] for k in range(4)]
        moved = poly([link_ref[4 * j + k] for k in range(4)], sent)
        s = [jnp.where(me > j, s[k] + moved[k], s[k]) for k in range(4)]
        e = [jnp.where(me < j, e[k] + moved[k], e[k]) for k in range(4)]
    moved = poly([link_ref[4 * blocks + k] for k in range(4)], s)
    first = 4 * levels * me
    after = [
        moved[k] + sent_ref[pl.ds(first + k, levels, stride=4), :] for k in range(4)
    ]
    back = return_map({key: link_ref[4 * blocks + 4 + m] for m, key in enumerate(COEFS)}, after)
    for k in range(4):
        enter_ref[pl.ds(k, levels, stride=8), :] = s[k]
        enter_ref[pl.ds(4 + k, levels, stride=8), :] = e[k] + back[k]
    corner = dot3(flat(extract_ref[...]), enter_ref[...], NT)
    here = lax.broadcasted_iota(jnp.int32, (N, N), 0) // 8 == lanes((N, N)) // 8
    corner = jnp.where(here, corner, 0.0)
    states = flat(base_ref[...]) + dot3(corner, flat(entry_ref[...]), NN)
    left = lanes((8, N)) < HALF
    for level in range(levels):
        own = states[8 * level:8 * level + 8]
        coefs = jnp.broadcast_to(coef_ref[level:level + 1, :], (8, N))
        out_ref[2 * level] = jnp.where(left, own, coefs)
        out_ref[2 * level + 1] = jnp.where(left, pltpu.roll(own, HALF, 1), coefs)


def run_groups(groups, size, reverse, maps, source, store, ends, starts):
    steps = range(size - 1, -1, -1) if reverse else range(size)
    total, state, kept = None, None, []
    for j in steps:
        kept.append((j, total, state))
        t, f = maps(j), source(j)
        state = f if state is None else [a + b for a, b in zip(poly(t, state), f)]
        total = t if total is None else poly(t, total)
    for k in range(4):
        ends[k], ends[4 + k] = total[k], state[k]
    enter = [jnp.zeros((1, N), F32)] * 4
    for c in range(groups - 1, -1, -1) if reverse else range(groups):
        row = slice(c, c + 1)
        for k in range(4):
            starts[k, row, :] = enter[k]
        moved = poly([ends[k, row, :] for k in range(4)], enter)
        enter = [moved[k] + ends[4 + k, row, :] for k in range(4)]
    enter = [starts[k] for k in range(4)]
    for j, total, state in kept:
        store(j, enter if total is None else [a + b for a, b in zip(poly(total, enter), state)])


def apply_y_kernel(states_ref, out_ref, packed, spread, links, returns, ends, starts):
    blocks = states_ref.shape[0] // 8
    groups = ends.shape[1]
    size = blocks // groups
    packed[...] = states_ref[pl.ds(0, blocks, stride=8), :]

    def coef(m):
        return jnp.broadcast_to(packed[:, HALF + m:HALF + m + 1], (blocks, N))

    for m in range(4):
        spread[m] = coef(m)

    def rows(j):
        return pl.ds(j, groups, stride=size)

    def store(first):
        def put(j, values):
            for k in range(4):
                links[first + k, rows(j), :] = values[k]

        return put

    def maps(j):
        return [spread[k, rows(j), :] for k in range(4)]

    for k in range(4):
        returns[k] = states_ref[pl.ds(k, blocks, stride=8), :]

    def source(j):
        return [returns[k, rows(j), :] for k in range(4)]

    run_groups(groups, size, False, maps, source, store(0), ends, starts)
    r = {key: coef(4 + m) for m, key in enumerate(COEFS)}
    back = return_map(r, [links[k] for k in range(4)])
    for k in range(4):
        returns[k] = back[k] + states_ref[pl.ds(4 + k, blocks, stride=8), :]
    run_groups(groups, size, True, maps, source, store(4), ends, starts)
    left = lanes((blocks, N)) < HALF
    for k in range(4):
        out_ref[pl.ds(k, blocks, stride=4), :] = jnp.where(
            left, links[k], pltpu.roll(links[4 + k], HALF, 1)
        )


def local_y_kernel(base_ref, enter_ref, entry_ref, filter_ref, out_ref):
    for level in range(out_ref.shape[0]):
        rows = base_ref[level] + dot3(enter_ref[level], entry_ref[level], TN)
        out_ref[level] = dot3(filter_ref[level], rows, NN)


def vertical_kernel(taps_ref, values_ref, entry_ref, out_ref, wide_ref):
    levels = out_ref.shape[0]
    turned = flat(entry_ref[...]).T
    owner = lanes((1, N)) // 8
    for level in range(levels):
        total, row = None, jnp.zeros((1, N), F32)
        for d in range(5):
            other = level + d - 2
            if 0 <= other < levels:
                term = taps_ref[d, level] * values_ref[other]
                total = term if total is None else total + term
                row = jnp.where(owner == other, taps_ref[d, level], row)
        out_ref[level] = total
        wide_ref[level] = wide_left(turned * row)


def final_kernel(values_ref, wide_ref, slots_ref, out_hbm, enter, whole, sems):
    levels = enter.shape[0]
    left = lanes((4, N)) < HALF
    for level in range(levels):
        a, b = slots_ref[2 * level], slots_ref[2 * level + 1]
        enter[level, 0:4, :] = jnp.where(left, a, pltpu.roll(b, HALF, 1))
        enter[level, 4:8, :] = jnp.where(left, pltpu.roll(a, HALF, 1), b)
    right = wide_right(flat(enter[...]))
    copies = []
    for level in range(0, levels, CHUNK):
        part = pl.ds(level, CHUNK)
        added = wide_dot(flat(wide_ref[part]), right).reshape(CHUNK, N, N)
        whole[part] = values_ref[part] + added
        if (level + CHUNK) % SENT == 0:
            part = pl.ds(level + CHUNK - SENT, SENT)
            copies.append(
                pltpu.make_async_copy(whole.at[part], out_hbm.at[part], sems.at[level // SENT])
            )
            copies[-1].start()
    for copy in copies:
        copy.wait()


VM = pl.BlockSpec(memory_space=pltpu.VMEM)
SM = pl.BlockSpec(memory_space=pltpu.SMEM)
HB = pl.BlockSpec(memory_space=pltpu.HBM)


def call(kernel, shapes, args, scratch=(), ins=None, out=VM, sems=0, types=None, grant=GRANT):
    types = types or [F32] * len(shapes)
    outs = [jax.ShapeDtypeStruct(shape, dtype) for shape, dtype in zip(shapes, types)]
    moved = 4 * sum(x.size for x in list(args) + outs)
    scratch = [pltpu.VMEM(shape, F32) for shape in scratch]
    if sems:
        scratch.append(pltpu.SemaphoreType.DMA((sems,)))
    return pl.pallas_call(
        kernel,
        out_shape=outs if len(outs) > 1 else outs[0],
        in_specs=ins or [VM] * len(args),
        out_specs=[out] * len(outs) if len(outs) > 1 else out,
        scratch_shapes=scratch,
        compiler_params=pltpu.CompilerParams(vmem_limit_bytes=grant),
        cost_estimate=pl.CostEstimate(flops=0, bytes_accessed=moved, transcendentals=0),
    )(*args)


def exchange(value, axis):
    return lax.all_to_all(value, axis, 0, 0, tiled=True)


def steps(control, scale_x, scale_y, taps):
    levels = control.shape[0]
    full, small = (levels, N, N), (levels, 8, N)
    nx, ny = lax.axis_size("gx"), lax.axis_size("gy")
    table = (N, levels, N)
    bind = functools.partial

    closing = call(
        states_x_kernel,
        [(nx, 4 * levels, N)],
        (scale_x, control),
        [(levels, N * nx), full, (N, N), (levels * nx // N, N, N)],
        ins=[HB, HB],
        sems=2,
        grant=60 << 20,
    )
    closing = exchange(closing, "gx")
    filter_x = call(bind(filter_kernel, "gx"), [(levels * N, N)], (scale_x,), [table, table])
    links = call(
        links_x_kernel,
        [(4 * nx + 4 + len(COEFS), levels, N)],
        (scale_x,),
        [(levels * nx // N, N, N)],
    )
    entry_x, gain_x, extract_y, entry_y, coefs = call(
        tables_kernel, [small, (levels, N), small, small, (levels, N)], (scale_x, scale_y)
    )
    local, base = call(
        local_x_kernel, [full, small], (control, gain_x, filter_x.reshape(full), extract_y)
    )

    slots, enter_x = call(
        states_y_kernel,
        [(ny, 8, N), (8 * levels, N)],
        (closing.reshape(4 * levels * nx, N), links, entry_x, extract_y, base, coefs),
    )
    enter_x = enter_x.reshape(small)
    slots = exchange(slots, "gy")
    filter_y = call(bind(filter_kernel, None), [(levels * N, N)], (scale_y,), [table, table])
    local = call(local_y_kernel, [full], (local, enter_x, entry_x, filter_y.reshape(full)))

    slots = call(
        apply_y_kernel,
        [(4 * ny, N)],
        (slots.reshape(8 * ny, N),),
        [(ny, N), (4, ny, N), (8, ny, N), (4, ny, N), (8, 8, N), (4, 8, N)],
    )
    slots = exchange(slots.reshape(ny, 4, N), "gy")
    local, wide = call(
        vertical_kernel,
        [full, (levels, N, 2 * N)],
        (taps, local, entry_y),
        ins=[SM, VM, VM],
        types=[F32, BF16],
    )
    return call(
        final_kernel, [full], (local, wide, slots), [small, full], out=HB, sems=levels // SENT
    )


def solution(mesh):
    return jax.shard_map(
        steps,
        mesh=mesh,
        in_specs=(P(None, "gy", "gx"), P(), P(None, "gy"), P()),
        out_specs=P(None, "gy", "gx"),
        check_vma=False,
    )
```
